32 devices in a mesh: ctx: 8 (over z, core), exp: 4 (over y, x).
Axes of the slice: x: 2, y: 2, z: 4, core: 2. Of those that a mesh axis runs over, the one named last changes fastest.
Arguments:
- queries: bfloat16 [4, 1024, 8192], P('exp', 'ctx'), may hold values from -64 to 64
- key_head_vectors: bfloat16 [4, 1024, 512], P('exp', 'ctx'), may hold values from -6 to 6
- value_head_vectors: bfloat16 [4, 1024, 512], P('exp', 'ctx'), may hold values from -6 to 6
- segment_ids: int32 [4, 1024], P('exp', 'ctx'), may hold values from 0 to 3, never falling along the last dimension, each value on 1 to 512 neighbouring positions
- normed: bfloat16 [4, 1024, 4096], P('exp', 'ctx'), may hold values from -6 to 6
- expert_ids: int32 [4, 1024, 2], P('exp', 'ctx'), may hold values from 0 to 3, all different within a row; in each aligned block of 128 rows (0 to 127, 128 to 255, ..., all dimensions but the last counted through in order) at most 80 rows name the same one
- gate_probs: float32 [4, 1024, 2], P('exp', 'ctx'), may hold values from 0.1 to 1
- gate_weight: bfloat16 [4, 768, 4096], P('exp', 'ctx'), may hold values from -0.09375 to 0.09375
- up_weight: bfloat16 [4, 768, 4096], P('exp', 'ctx'), may hold values from -0.09375 to 0.09375
- down_weight: bfloat16 [4, 768, 4096], P('exp', 'ctx'), may hold values from -0.21875 to 0.21875
Outputs:
- context: bfloat16 [4, 1024, 8192], P('exp', 'ctx')
- expert_mix: bfloat16 [4, 1024, 4096], P('exp', 'ctx')
The draws below stay inside these ranges and needn't reach their ends.
Inputs may be any that keep to these rules, and one draw needn't show every extreme that they name: `segment_ids`: ids never fall along a sequence; an even id marks a document, an odd id the question that reads the document just before it; each segment holds at most 512 positions and one holds exactly that many. `expert_ids`: each position names 2 different experts. Within the rows of one device no expert is named more than 80 times, a bound that some block reaches.
All inputs are finite; a program needn't handle non-finite values.
Results may differ from the reference program's by a relative error of at most 0.0058.
Values may be sent and summed in bfloat16 or wider, within the bound.
A program may use at most 128 MiB of HBM per device.

```python
import math
import jax
import jax.numpy as jnp
import numpy as np
from jax import lax

D = 4096
QUERY_HEAD_COUNT = 64
KEY_HEAD_COUNT = 4
HEAD_SIZE = 128
FF = 768
TOPK = 2
TOK_DEV = 128
EXPERTS = 4
SEQUENCE_LENGTH = 1024
SEQUENCE_COUNT = 4
CAP = 80
N_CTX = 8


def draw_pairs(key):
    start_offset = jax.random.fold_in(key, 7)
    query_result = jnp.clip(jax.random.normal(jax.random.fold_in(start_offset, 1), (SEQUENCE_COUNT, SEQUENCE_LENGTH, QUERY_HEAD_COUNT, HEAD_SIZE), jnp.float32), -6.0, 6.0)
    key_result = jnp.clip(jax.random.normal(jax.random.fold_in(start_offset, 2), (SEQUENCE_COUNT, SEQUENCE_LENGTH, KEY_HEAD_COUNT, HEAD_SIZE), jnp.float32), -6.0, 6.0)
    return (query_result.reshape(SEQUENCE_COUNT, SEQUENCE_LENGTH, QUERY_HEAD_COUNT * HEAD_SIZE), key_result.reshape(SEQUENCE_COUNT, SEQUENCE_LENGTH, KEY_HEAD_COUNT * HEAD_SIZE))


def draw_queries(key, part):
    return draw_pairs(key)[0].astype(jnp.bfloat16)


def draw_key_head_vectors(key, part):
    return draw_pairs(key)[1].astype(jnp.bfloat16)


def level_of(key, dims, pieces, smallest, top_value):
    level, own = 1.0, jax.random.fold_in(key, 6)
    for axis_at, blocks in pieces:
        steps = jnp.exp(jax.random.uniform(jax.random.fold_in(own, axis_at), (blocks,), jnp.float32, smallest / len(pieces), top_value / len(pieces)))
        level = level * jnp.repeat(steps, dims[axis_at] // blocks).reshape([-1 if axis == axis_at else 1 for axis in range(len(dims))])
    return level


def length_profile(count, total, most, skew):
    weights = [(1 << 20) // math.isqrt(standing ** skew) + 1 for standing in range(2, count + 1)]
    spare, holding = total - most - (count - 1), [1] * (count - 1)
    while spare > 0:
        movable = [i for i in range(count - 1) if holding[i] < most]
        mass, remaining = sum([weights[i] for i in movable]), spare
        for i in movable:
            more = min(most - holding[i], max(1, remaining * weights[i] // mass), spare)
            holding[i] = holding[i] + more
            spare = spare - more
    return np.array([most] + holding)


def ragged_sizes(key, number_of, total, most, skew):
    if number_of == 2:
        one = jax.random.randint(key, (), max(1, total - most), min(most, total - 1) + 1)
        return jnp.stack([one, total - one])
    tallies = jnp.asarray(length_profile(number_of, total, most, skew), jnp.int32)
    twos = (number_of - 1) // 2
    donor, receiver = tallies[1:1 + 2 * twos:2], tallies[2:2 + 2 * twos:2]
    room = jnp.minimum(donor - 1, most - receiver)
    moved = jax.random.randint(jax.random.fold_in(key, 1), (twos,), 0, 1 << 20) % (room + 1)
    tallies = tallies.at[1:1 + 2 * twos:2].set(donor - moved).at[2:2 + 2 * twos:2].set(receiver + moved)
    return tallies[jax.random.permutation(jax.random.fold_in(key, 2), number_of)]


def deal_out(stream_key, own, number, rows, count, top, limit, skew):
    order = jax.random.permutation(stream_key, count)
    crowded, ordinary = load_shares(count, rows * top, limit, skew, True), load_shares(count, rows * top, limit, skew, False)
    places = jnp.arange(count)

    def named(lengths, rotation):
        used = int((lengths > 0).sum())
        fixed = max(1, used // 4)
        shifted = fixed + (places - fixed + rotation * (used - fixed)) % max(1, count - fixed)
        return jnp.zeros((count,), jnp.int32).at[order[jnp.where(places < fixed, places, shifted)]].set(jnp.asarray(lengths, jnp.int32))

    lengths = jnp.where(number % 4 == 0, named(crowded, number // 4), named(ordinary, number - number // 4 - 1))
    mixed = jax.random.permutation(jax.random.fold_in(own, 3), count)
    source_of, sink = mixed[0:count // 2 * 2:2], mixed[1:count // 2 * 2:2]
    room = jnp.minimum(lengths[source_of] - 1, limit - lengths[sink]) // 2
    room = jnp.where((source_of == order[0]) | (sink == order[0]) | (lengths[sink] == 0), 0, jnp.maximum(room, 0))
    shifted = jax.random.randint(jax.random.fold_in(own, 4), (count // 2,), 0, 1 << 20) % (room + 1)
    lengths = lengths.at[source_of].add(-shifted).at[sink].add(shifted)
    items = jnp.searchsorted(jnp.cumsum(lengths), jnp.arange(rows * top), side="right").astype(jnp.int32)
    table = items.reshape(top, rows).T
    table = table[jax.random.permutation(jax.random.fold_in(own, 1), rows)]
    rotation = jax.random.randint(jax.random.fold_in(own, 2), (rows, 1), 0, top)
    return jnp.take_along_axis(table, (jnp.arange(top)[None, :] + rotation) % top, axis=1)


def load_shares(number_of, total, reach, skew, full):
    loads = [(1 << 20) // math.isqrt(standing ** skew) + 1 for standing in range(1, number_of + 1)]
    largest = reach if full else min(reach, max(-(-total // number_of), total * loads[0] // sum(loads)))
    least = 1 if total - largest >= number_of - 1 else 0
    given, spare = [largest] + [least] * (number_of - 1), total - largest - least * (number_of - 1)
    while spare > 0:
        free = [i for i in range(1, number_of) if given[i] < largest] or [i for i in range(1, number_of) if given[i] < reach]
        mass, left = sum([loads[i] for i in free]), spare
        for i in free:
            extra = min(reach - given[i], max(1, left * loads[i] // mass), spare)
            given[i] = given[i] + extra
            spare = spare - extra
    return np.array(given)


def scatter_about(key, extent, scale, reach, cuts=(), held_as=jnp.bfloat16):
    drawn = scale * jax.random.normal(key, extent, jnp.float32)
    if cuts:
        drawn = drawn * level_of(key, extent, cuts, -0.22, 0.18)
    return jnp.clip(drawn, -reach, reach).astype(held_as)


def setup_inputs(seed: int = 0) -> dict:
    key_list = jax.random.split(jax.random.key(seed), 11)
    queries = draw_queries(jax.random.fold_in(key_list[10], 71), 0)
    key_head_vectors = draw_key_head_vectors(jax.random.fold_in(key_list[10], 71), 0)
    value_head_vectors = scatter_about(key_list[2], (SEQUENCE_COUNT, SEQUENCE_LENGTH, KEY_HEAD_COUNT * HEAD_SIZE), 1.0, 6.0, ((0, 4), (1, 8)))
    segment_ids = jax.vmap(lambda own: jnp.searchsorted(jnp.cumsum(ragged_sizes(own, 4, SEQUENCE_LENGTH, SEQUENCE_LENGTH // 2, 1)), jnp.arange(SEQUENCE_LENGTH), side="right"))(jax.random.split(key_list[3], SEQUENCE_COUNT)).reshape((SEQUENCE_COUNT, SEQUENCE_LENGTH)).astype(jnp.int32)
    normed = scatter_about(key_list[4], (SEQUENCE_COUNT, SEQUENCE_LENGTH, D), 1.0, 6.0, ((0, 4), (1, 8)))
    expert_ids_keys = jax.random.split(jax.random.fold_in(key_list[5], 1), SEQUENCE_COUNT * SEQUENCE_LENGTH // TOK_DEV)
    expert_ids_turns = jax.random.permutation(jax.random.fold_in(key_list[5], 3), SEQUENCE_COUNT * SEQUENCE_LENGTH // TOK_DEV)
    expert_ids = jax.vmap(lambda own, number: deal_out(jax.random.fold_in(key_list[5], 2), own, number, TOK_DEV, EXPERTS, TOPK, CAP, 2))(expert_ids_keys, expert_ids_turns).reshape((SEQUENCE_COUNT, SEQUENCE_LENGTH, TOPK))
    gate_probs = jnp.clip(0.1 + 0.9 * jax.random.uniform(key_list[6], (SEQUENCE_COUNT, SEQUENCE_LENGTH, TOPK), jnp.float32) ** level_of(key_list[6], (SEQUENCE_COUNT, SEQUENCE_LENGTH, TOPK), ((0, 4), (1, 8)), -0.2, 0.2), 0.1, 1.0)
    gate_weight = scatter_about(key_list[7], (EXPERTS, FF, D), D ** -0.5, 0.09375, ((0, 4), (1, 8)))
    up_weight = scatter_about(key_list[8], (EXPERTS, FF, D), D ** -0.5, 0.09375, ((0, 4), (1, 8)))
    down_weight = scatter_about(key_list[9], (EXPERTS, FF, D), FF ** -0.5, 0.21875, ((0, 4), (1, 8)))
    return dict(queries=queries, key_head_vectors=key_head_vectors, value_head_vectors=value_head_vectors, segment_ids=segment_ids, normed=normed, expert_ids=expert_ids, gate_probs=gate_probs, gate_weight=gate_weight, up_weight=up_weight, down_weight=down_weight)


def attend_mask(query_places, key_places, query_segments, key_segments):
    causal = key_places[None, :] <= query_places[:, None]
    same_segment = key_segments[None, :] == query_segments[:, None]
    source = (query_segments[:, None] % 2 == 1) & (key_segments[None, :] == query_segments[:, None] - 1)
    return causal & (same_segment | source)


def attend_sequence(operands):
    queries, key_head_vectors, value_head_vectors, segment_ids = operands
    span_length = queries.shape[0]
    query_group_count = QUERY_HEAD_COUNT // KEY_HEAD_COUNT
    query_head_rows = queries.astype(jnp.float32).reshape(span_length, KEY_HEAD_COUNT, query_group_count, HEAD_SIZE).transpose(1, 2, 0, 3)
    key_head_rows = key_head_vectors.astype(jnp.float32).reshape(span_length, KEY_HEAD_COUNT, HEAD_SIZE).transpose(1, 0, 2)
    value_head_rows = value_head_vectors.astype(jnp.float32).reshape(span_length, KEY_HEAD_COUNT, HEAD_SIZE).transpose(1, 0, 2)
    places = jnp.arange(span_length, dtype=jnp.int32)
    allowed = attend_mask(places, places, segment_ids, segment_ids)

    def per_head(parts):
        query_block, key_block, value_block = parts
        scores = jnp.einsum("gqd,kd->gqk", query_block, key_block) * (HEAD_SIZE ** -0.5)
        masked = jnp.where(allowed[None], scores, -1e30)
        row_peak = jnp.max(masked, axis=-1, keepdims=True)
        exponent = jnp.where(allowed[None], jnp.exp(masked - row_peak), 0.0)
        row_total = jnp.sum(exponent, axis=-1, keepdims=True)
        rounded = lax.optimization_barrier((exponent / row_total).astype(jnp.bfloat16))
        return jnp.einsum("gqk,kd->gqd", rounded.astype(jnp.float32), value_block).astype(jnp.bfloat16)

    heads_out = lax.map(per_head, (query_head_rows, key_head_rows, value_head_rows))
    return heads_out.transpose(2, 0, 1, 3).reshape(span_length, QUERY_HEAD_COUNT * HEAD_SIZE)


def reference(queries, key_head_vectors, value_head_vectors, segment_ids, normed, expert_ids, gate_probs, gate_weight, up_weight, down_weight):
    context = lax.map(attend_sequence, (queries, key_head_vectors, value_head_vectors, segment_ids))
    tokens = normed.reshape(SEQUENCE_COUNT * SEQUENCE_LENGTH, D)
    flat_ids = expert_ids.reshape(SEQUENCE_COUNT * SEQUENCE_LENGTH * TOPK).astype(jnp.int32)
    assigned = SEQUENCE_COUNT * SEQUENCE_LENGTH * TOPK
    owners = jnp.arange(assigned, dtype=jnp.int32) // TOPK
    sorted_order = jnp.argsort(flat_ids, stable=True).astype(jnp.int32)
    expert_range = jnp.arange(EXPERTS, dtype=jnp.int32)
    counts = jnp.sum((flat_ids[None, :] == expert_range[:, None]).astype(jnp.int32), axis=1)
    starts = jnp.sum((flat_ids[None, :] < expert_range[:, None]).astype(jnp.int32), axis=1)
    most_load = SEQUENCE_COUNT * N_CTX * CAP
    padded_order = jnp.concatenate([sorted_order, jnp.zeros((most_load,), jnp.int32)])
    flat_gates = gate_probs.reshape(assigned).astype(jnp.float32)

    def add_expert(running, expert):
        picked_rows = lax.dynamic_slice_in_dim(padded_order, starts[expert], most_load)
        live_slot = jnp.arange(most_load, dtype=jnp.int32) < counts[expert]
        token_rows = owners[picked_rows]
        inputs = tokens[token_rows]
        gate_part = jnp.dot(inputs, gate_weight[expert].T, preferred_element_type=jnp.float32)
        up_part = jnp.dot(inputs, up_weight[expert].T, preferred_element_type=jnp.float32)
        activation = (jax.nn.silu(gate_part) * up_part).astype(jnp.bfloat16)
        result = jnp.dot(activation, down_weight[expert], preferred_element_type=jnp.float32).astype(jnp.bfloat16)
        gate_scale = jnp.where(live_slot, flat_gates[picked_rows], 0.0)
        return running.at[token_rows].add(gate_scale[:, None] * result.astype(jnp.float32)), None

    blended, unused = lax.scan(add_expert, jnp.zeros((SEQUENCE_COUNT * SEQUENCE_LENGTH, D), jnp.float32), expert_range)
    expert_mix = blended.astype(jnp.bfloat16).reshape(SEQUENCE_COUNT, SEQUENCE_LENGTH, D)
    return (context, expert_mix)
```

```python
import functools
import math

import jax
import jax.numpy as jnp
from jax import lax
from jax.experimental import pallas as pl
from jax.experimental.pallas import tpu as pltpu
from jax.sharding import PartitionSpec as P

KEY_HEAD_COUNT = 4
HEAD_SIZE = 128
COLUMN_BLOCKS = 4
HEADS_AT_ONCE = 4
MESH = pl.DeviceIdType.MESH
F32 = jnp.float32
BF16 = jnp.bfloat16


def kernel(
    n_ctx, n_exp, cap,
    q_hbm, k_hbm, v_hbm, seg_in, x_in, ids_in, prob_in, gate_hbm, up_hbm, down_hbm,
    ctx_out, mix_out,
    q_buf, k_buf, v_buf, seg_buf, bias, ctx_buf, weights, rows_out, rows_in,
    total, result, returned, pick, gates, mix_buf,
    local_sem, kv_send, kv_swap, kv_recv, w_left, w_right, w_swap, w_recv,
    x_send, x_recv, r_send, r_recv, out_sem,
):
    me = lax.axis_index("ctx")
    mine = lax.axis_index("exp")
    n_z = n_ctx // 2
    z, core = me // 2, me % 2
    mate = me + 1 - 2 * core
    tokens, width = x_in.shape
    group = q_buf.shape[1] // (KEY_HEAD_COUNT * HEAD_SIZE)
    span = n_ctx * tokens

    def send(src, dst, send_sem, recv_sem, where):
        return pltpu.make_async_remote_copy(
            src_ref=src, dst_ref=dst, send_sem=send_sem, recv_sem=recv_sem,
            device_id=where, device_id_type=MESH,
        )

    def key_rows(slot):
        return pl.ds(pl.multiple_of(slot * tokens, tokens), tokens)

    own_weights = (gate_hbm, up_hbm, down_hbm)
    own_kv = (k_hbm, v_hbm, seg_in)

    def kv_slot(j, slot):
        return seg_buf.at[slot] if j == 2 else (k_buf, v_buf)[j].at[key_rows(slot)]

    barrier = pltpu.get_barrier_semaphore()
    for d in range(1, n_z):
        pl.semaphore_signal(barrier, inc=1, device_id={"ctx": (z + d) % n_z * 2 + core}, device_id_type=MESH)
    pl.semaphore_signal(barrier, inc=1, device_id={"ctx": mate}, device_id_type=MESH)
    for d in range(1, n_exp):
        pl.semaphore_signal(barrier, inc=1, device_id={"exp": (mine + d) % n_exp}, device_id_type=MESH)
    pl.semaphore_wait(barrier, n_z - 1 + 1 + n_exp - 1)

    def kv_out(d, j):
        there = (z + d) % n_z
        return send(own_kv[j], kv_slot(j, me), kv_send.at[there, j], kv_recv.at[me, j], {"ctx": there * 2 + core})

    def kv_pass(d, j):
        slot = (z + d) % n_z * 2 + core
        src = own_kv[j] if d == 0 else kv_slot(j, slot)
        return send(src, kv_slot(j, slot), kv_swap.at[slot // 2, j], kv_recv.at[slot, j], {"ctx": mate})

    for d in range(1, n_z):
        for j in range(3):
            kv_out(d, j).start()
    for j in range(3):
        kv_pass(0, j).start()

    def w_side(side, src, origin, slot, k):
        step = 2 if side else -2
        sem = w_right if side else w_left
        return send(src, weights.at[k, slot], sem.at[origin, k], w_recv.at[slot, k], {"ctx": me + step})

    def w_mate(src, origin, slot, k):
        return send(src, weights.at[k, slot], w_swap.at[origin, k], w_recv.at[slot, k], {"ctx": mate})

    def has_side(side):
        return z + 1 < n_z if side else z > 0

    for k in range(3):
        for side in (0, 1):
            @pl.when(has_side(side))
            def _():
                w_side(side, own_weights[k], z, me, k).start()
        w_mate(own_weights[k], z, me, k).start()

    local = [pltpu.make_async_copy(own_weights[k], weights.at[k, me], local_sem.at[k]) for k in range(3)]
    local += [pltpu.make_async_copy(own_kv[j], kv_slot(j, me), local_sem.at[3 + j]) for j in range(3)]
    local += [pltpu.make_async_copy(q_hbm, q_buf, local_sem.at[6])]
    for copy in local:
        copy.start()

    t_row = lax.broadcasted_iota(jnp.int32, (tokens, tokens), 0)
    t_col = lax.broadcasted_iota(jnp.int32, (tokens, tokens), 1)

    def as_row(column):
        return jnp.sum(jnp.where(t_row == t_col, column, 0), axis=0, keepdims=True)

    ids = ids_in[...]
    probs = prob_in[...]
    id0, id1 = ids[:, 0:1], ids[:, 1:2]
    e_col = lax.broadcasted_iota(jnp.int32, (tokens, n_exp), 1)
    e_row = lax.broadcasted_iota(jnp.int32, (n_exp, tokens), 0)
    named_col = jnp.where((e_col == id0) | (e_col == id1), 1.0, 0.0).astype(F32)
    named_row = jnp.where((e_row == as_row(id0)) | (e_row == as_row(id1)), 1.0, 0.0).astype(F32)
    before = jnp.where(t_col < t_row, 1.0, 0.0).astype(BF16)
    after = jnp.where(t_row < t_col, 1.0, 0.0).astype(BF16)
    rank_col = jnp.dot(before, named_col.astype(BF16), preferred_element_type=F32)
    rank_row = jnp.dot(named_row.astype(BF16), after, preferred_element_type=F32)
    weight_col = jnp.where(e_col == id0, probs[:, 0:1], 0.0) + jnp.where(e_col == id1, probs[:, 1:2], 0.0)
    place_row = lax.broadcasted_iota(jnp.int32, (cap, tokens), 0).astype(F32)
    place_col = lax.broadcasted_iota(jnp.int32, (tokens, cap), 1).astype(F32)
    x = x_in[...]
    for e in range(n_exp):
        chosen = jnp.where(place_row == rank_row[e : e + 1, :], named_row[e : e + 1, :], 0.0)
        rows_out[e] = jnp.dot(chosen.astype(BF16), x, preferred_element_type=F32).astype(BF16)
        back = jnp.where(place_col == rank_col[:, e : e + 1], named_col[:, e : e + 1], 0.0)
        pick[e] = back.astype(BF16)
        gates[e] = weight_col[:, e : e + 1]

    def x_out(d):
        there = (mine + d) % n_exp
        return send(rows_out.at[there], rows_in.at[mine], x_send.at[there], x_recv.at[mine], {"exp": there})

    def x_arrival(d):
        source = (mine + d) % n_exp
        return send(rows_out.at[source], rows_in.at[source], x_send.at[source], x_recv.at[source], {"exp": source})

    for d in range(1, n_exp):
        x_out(d).start()
    rows_in[mine] = rows_out[mine]

    for d in range(1, n_z):
        for j in range(3):
            kv_pass(d, j).wait_recv()
            kv_pass(d, j).start()

    def kv_from_mate(d, j):
        slot = (z + d) % n_z * 2 + 1 - core
        return send(kv_slot(j, slot), kv_slot(j, slot), kv_swap.at[slot // 2, j], kv_recv.at[slot, j], {"ctx": mate})

    for d in range(n_z):
        for j in range(3):
            kv_from_mate(d, j).wait_recv()
    for copy in local[3:]:
        copy.wait()

    own_segment = jnp.sum(
        jnp.where(t_row == t_col, jnp.broadcast_to(seg_buf[me], (tokens, tokens)), 0), axis=1, keepdims=True
    )
    source_segment = jnp.where(own_segment % 2 == 1, own_segment - 1, own_segment)
    for c in range(n_ctx):
        theirs = seg_buf[c]
        allowed = (t_col + c * tokens <= t_row + me * tokens) & (
            (theirs == own_segment) | (theirs == source_segment)
        )
        bias[:, c * tokens : (c + 1) * tokens] = jnp.where(allowed, 0.0, -1e30)

    def relay(s, k):
        for side in (0, 1):
            origin = z - s if side else z + s
            slot = origin * 2 + core

            @pl.when((origin >= 0) & (origin < n_z))
            def _():
                here = weights.at[k, slot]
                w_mate(here, origin, slot, k).wait_recv()

                @pl.when(has_side(side))
                def _():
                    w_side(side, here, origin, slot, k).start()

                w_mate(here, origin, slot, k).start()

    scale = HEAD_SIZE ** -0.5 * math.log2(math.e)

    def attend(g, carry):
        lanes = pl.ds(pl.multiple_of(g * HEAD_SIZE, HEAD_SIZE), HEAD_SIZE)

        def heads(i, inner):
            for u in range(HEADS_AT_ONCE):
                head = g * group + i * HEADS_AT_ONCE + u
                at = pl.ds(pl.multiple_of(head * HEAD_SIZE, HEAD_SIZE), HEAD_SIZE)
                scores = lax.dot_general(
                    q_buf[:, at], k_buf[:, lanes], (((1,), (1,)), ((), ())), preferred_element_type=F32
                )
                scores = scores * scale + bias[...]
                peak = jnp.max(scores, axis=1, keepdims=True)
                power = jnp.exp2(scores - peak)
                share = 1.0 / jnp.sum(power, axis=1, keepdims=True)
                ctx_buf[:, at] = jnp.dot(
                    (power * share).astype(BF16), v_buf[:, lanes], preferred_element_type=F32
                ).astype(BF16)
            return inner

        lax.fori_loop(0, group // HEADS_AT_ONCE, heads, 0)

        @pl.when(g < 3)
        def _():
            relay(1, g)

        return carry

    lax.fori_loop(0, KEY_HEAD_COUNT, attend, 0)
    ctx_copy = pltpu.make_async_copy(ctx_buf, ctx_out, out_sem.at[0])
    ctx_copy.start()

    for d in range(1, n_exp):
        x_arrival(d).wait_recv()
    for copy in local[:3]:
        copy.wait()
    columns = width // COLUMN_BLOCKS

    def block(cb):
        return pl.ds(pl.multiple_of(cb * columns, columns), columns)

    total[...] = jnp.zeros_like(total)

    def hidden_of(origin):
        other = origin * 2 + 1 - core
        for k in range(3):
            w_mate(weights.at[k, other], origin, other, k).wait_recv()
        inputs = rows_in[...].reshape(n_exp * cap, width)
        both = pl.ds(origin * 2, 2)
        gate_w = weights[0, both].reshape(-1, width)
        up_w = weights[1, both].reshape(-1, width)
        gate = lax.dot_general(inputs, gate_w, (((1,), (1,)), ((), ())), preferred_element_type=F32)
        up = lax.dot_general(inputs, up_w, (((1,), (1,)), ((), ())), preferred_element_type=F32)
        hidden = (gate / (1.0 + jnp.exp(-gate)) * up).astype(BF16)

        def down(cb, carry):
            at = block(cb)
            down_w = weights[2, both, :, at].reshape(-1, columns)
            total[:, at] += jnp.dot(hidden, down_w, preferred_element_type=F32)
            return carry

        lax.fori_loop(0, COLUMN_BLOCKS, down, 0)

    hidden_of(z)

    def far(s, carry):
        @pl.when(s > 1)
        def _():
            for k in range(3):
                relay(s, k)

        def one(side, inner):
            origin = z + s - 2 * s * side

            @pl.when((origin >= 0) & (origin < n_z))
            def _():
                hidden_of(origin)

            return inner

        lax.fori_loop(0, 2, one, 0)
        return carry

    lax.fori_loop(1, n_z, far, 0)

    def r_out(d, cb):
        there = (mine + d) % n_exp
        at = pl.ds(cb * columns, columns)
        return send(
            result.at[there, :, at], returned.at[mine, :, at],
            r_send.at[there, cb], r_recv.at[mine, cb], {"exp": there},
        )

    def r_arrival(d, cb):
        source = (mine + d) % n_exp
        at = pl.ds(cb * columns, columns)
        return send(
            result.at[source, :, at], returned.at[source, :, at],
            r_send.at[source, cb], r_recv.at[source, cb], {"exp": source},
        )

    for cb in range(COLUMN_BLOCKS):
        at = pl.ds(cb * columns, columns)
        result[:, :, at] = total[:, at].astype(BF16).reshape(n_exp, cap, columns)
        for d in range(1, n_exp):
            r_out(d, cb).start()
    for cb in range(COLUMN_BLOCKS):
        at = pl.ds(cb * columns, columns)
        mix = gates[mine] * jnp.dot(pick[mine], result[mine, :, at], preferred_element_type=F32)
        for d in range(1, n_exp):
            r_arrival(d, cb).wait_recv()
            source = (mine + d) % n_exp
            mix += gates[source] * jnp.dot(pick[source], returned[source, :, at], preferred_element_type=F32)
        mix_buf[:, at] = mix.astype(BF16)
    mix_copy = pltpu.make_async_copy(mix_buf, mix_out, out_sem.at[1])
    mix_copy.start()

    for d in range(1, n_z):
        for j in range(3):
            kv_out(d, j).wait_send()
    for d in range(n_z):
        for j in range(3):
            kv_pass(d, j).wait_send()
    for k in range(3):
        for side in (0, 1):
            @pl.when(has_side(side))
            def _():
                w_side(side, own_weights[k], z, me, k).wait_send()
        w_mate(own_weights[k], z, me, k).wait_send()

    def sent(s, carry):
        for k in range(3):
            for side in (0, 1):
                origin = z - s if side else z + s
                slot = origin * 2 + core

                @pl.when((origin >= 0) & (origin < n_z))
                def _():
                    here = weights.at[k, slot]

                    @pl.when(has_side(side))
                    def _():
                        w_side(side, here, origin, slot, k).wait_send()

                    w_mate(here, origin, slot, k).wait_send()
        return carry

    lax.fori_loop(1, n_z, sent, 0)
    for d in range(1, n_exp):
        x_out(d).wait_send()
        for cb in range(COLUMN_BLOCKS):
            r_out(d, cb).wait_send()
    ctx_copy.wait()
    mix_copy.wait()


def on_device(
    n_ctx, n_exp,
    queries, key_head_vectors, value_head_vectors, segment_ids,
    normed, expert_ids, gate_probs, gate_weight, up_weight, down_weight,
):
    tokens, q_width = queries.shape[1:]
    kv_width = key_head_vectors.shape[2]
    width = normed.shape[2]
    hidden = gate_weight.shape[1]
    most = tokens * expert_ids.shape[2] * 5 // (4 * n_exp)
    cap = -(-most // 16) * 16
    span = n_ctx * tokens
    n_z = n_ctx // 2
    dma = pltpu.SemaphoreType.DMA
    hbm = pl.BlockSpec(memory_space=pl.ANY)
    vmem = pl.BlockSpec(memory_space=pltpu.VMEM)
    context, mixture = pl.pallas_call(
        functools.partial(kernel, n_ctx, n_exp, cap),
        out_shape=(
            jax.ShapeDtypeStruct((tokens, q_width), BF16),
            jax.ShapeDtypeStruct((tokens, width), BF16),
        ),
        in_specs=[hbm, hbm, hbm, vmem, vmem, vmem, vmem, hbm, hbm, hbm],
        out_specs=(hbm, hbm),
        scratch_shapes=[
            pltpu.VMEM((tokens, q_width), BF16),
            pltpu.VMEM((span, kv_width), BF16),
            pltpu.VMEM((span, kv_width), BF16),
            pltpu.VMEM((n_ctx, 1, tokens), jnp.int32),
            pltpu.VMEM((tokens, span), F32),
            pltpu.VMEM((tokens, q_width), BF16),
            pltpu.VMEM((3, n_ctx, hidden, width), BF16),
            pltpu.VMEM((n_exp, cap, width), BF16),
            pltpu.VMEM((n_exp, cap, width), BF16),
            pltpu.VMEM((n_exp * cap, width), F32),
            pltpu.VMEM((n_exp, cap, width), BF16),
            pltpu.VMEM((n_exp, cap, width), BF16),
            pltpu.VMEM((n_exp, tokens, cap), BF16),
            pltpu.VMEM((n_exp, tokens, 1), F32),
            pltpu.VMEM((tokens, width), BF16),
            dma((7,)),
            dma((n_z, 3)),
            dma((n_z, 3)),
            dma((n_ctx, 3)),
            dma((n_z, 3)),
            dma((n_z, 3)),
            dma((n_z, 3)),
            dma((n_ctx, 3)),
            dma((n_exp,)),
            dma((n_exp,)),
            dma((n_exp, COLUMN_BLOCKS)),
            dma((n_exp, COLUMN_BLOCKS)),
            dma((2,)),
        ],
        compiler_params=pltpu.CompilerParams(
            collective_id=0, has_side_effects=True, vmem_limit_bytes=60 * 1024 * 1024
        ),
        name="layer",
    )(
        queries[0], key_head_vectors[0], value_head_vectors[0], segment_ids,
        normed[0], expert_ids[0], gate_probs[0], gate_weight[0], up_weight[0], down_weight[0],
    )
    return context[None], mixture[None]


def solution(mesh):
    rows = P("exp", "ctx", None)
    in_specs = (rows, rows, rows, P("exp", "ctx"), rows, rows, rows, rows, rows, rows)
    return jax.shard_map(
        functools.partial(on_device, mesh.shape["ctx"], mesh.shape["exp"]),
        mesh=mesh, in_specs=in_specs, out_specs=(rows, rows), check_vma=False,
    )
```

```python
import functools
import math

import jax
import jax.numpy as jnp
from jax import lax
from jax.experimental import pallas as pl
from jax.experimental.pallas import tpu as pltpu
from jax.sharding import PartitionSpec as P

KEY_HEAD_COUNT = 4
HEAD_SIZE = 128
COLUMN_BLOCKS = 4
HEADS_AT_ONCE = 4
PIECES = 2 + COLUMN_BLOCKS
MESH = pl.DeviceIdType.MESH
F32 = jnp.float32
BF16 = jnp.bfloat16


def kernel(
    n_ctx, n_exp, cap,
    q_hbm, k_hbm, v_hbm, seg_in, x_in, ids_in, prob_in, gate_hbm, up_hbm, down_hbm,
    ctx_out, mix_out,
    q_buf, k_buf, v_buf, seg_buf, bias, ctx_buf, weights, rows_out, rows_in,
    hidden, hidden_all, result, returned, pick, gates, mix_buf,
    local_sem, kv_send, kv_swap, kv_recv, w_left, w_right, w_swap, w_recv,
    x_send, x_recv, r_send, r_recv, out_sem,
):
    me = lax.axis_index("ctx")
    mine = lax.axis_index("exp")
    n_z = n_ctx // 2
    z, core = me // 2, me % 2
    mate = me + 1 - 2 * core
    tokens, width = x_in.shape
    group = q_buf.shape[1] // (KEY_HEAD_COUNT * HEAD_SIZE)
    span = n_ctx * tokens

    def send(src, dst, send_sem, recv_sem, where):
        return pltpu.make_async_remote_copy(
            src_ref=src, dst_ref=dst, send_sem=send_sem, recv_sem=recv_sem,
            device_id=where, device_id_type=MESH,
        )

    def key_rows(slot):
        return pl.ds(pl.multiple_of(slot * tokens, tokens), tokens)

    own_weights = (gate_hbm, up_hbm, down_hbm)
    columns = width // COLUMN_BLOCKS

    def block(cb):
        return pl.ds(pl.multiple_of(cb * columns, columns), columns)

    def own_piece(k):
        return own_weights[k] if k < 2 else down_hbm.at[:, block(k - 2)]

    def piece(k, slot):
        return weights.at[k, slot] if k < 2 else weights.at[2, slot, :, block(k - 2)]

    own_kv = (k_hbm, v_hbm, seg_in)

    def kv_slot(j, slot):
        return seg_buf.at[slot] if j == 2 else (k_buf, v_buf)[j].at[key_rows(slot)]

    barrier = pltpu.get_barrier_semaphore()
    for d in range(1, n_z):
        pl.semaphore_signal(barrier, inc=1, device_id={"ctx": (z + d) % n_z * 2 + core}, device_id_type=MESH)
    pl.semaphore_signal(barrier, inc=1, device_id={"ctx": mate}, device_id_type=MESH)
    for d in range(1, n_exp):
        pl.semaphore_signal(barrier, inc=1, device_id={"exp": (mine + d) % n_exp}, device_id_type=MESH)
    pl.semaphore_wait(barrier, n_z - 1 + 1 + n_exp - 1)

    def kv_out(d, j):
        there = (z + d) % n_z
        return send(own_kv[j], kv_slot(j, me), kv_send.at[there, j], kv_recv.at[me, j], {"ctx": there * 2 + core})

    def kv_pass(d, j):
        slot = (z + d) % n_z * 2 + core
        src = own_kv[j] if d == 0 else kv_slot(j, slot)
        return send(src, kv_slot(j, slot), kv_swap.at[slot // 2, j], kv_recv.at[slot, j], {"ctx": mate})

    for d in range(1, n_z):
        for j in range(3):
            kv_out(d, j).start()
    for j in range(3):
        kv_pass(0, j).start()

    def w_side(side, src, origin, slot, k):
        step = 2 if side else -2
        sem = w_right if side else w_left
        return send(src, piece(k, slot), sem.at[origin, k], w_recv.at[slot, k], {"ctx": me + step})

    def w_mate(src, origin, slot, k):
        return send(src, piece(k, slot), w_swap.at[origin, k], w_recv.at[slot, k], {"ctx": mate})

    def has_side(side):
        return z + 1 < n_z if side else z > 0

    def share_own(k):
        for side in (0, 1):
            @pl.when(has_side(side))
            def _():
                w_side(side, own_piece(k), z, me, k).start()
        w_mate(own_piece(k), z, me, k).start()

    for k in range(2):
        share_own(k)

    local = [pltpu.make_async_copy(own_weights[k], weights.at[k, me], local_sem.at[k]) for k in range(3)]
    local += [pltpu.make_async_copy(own_kv[j], kv_slot(j, me), local_sem.at[3 + j]) for j in range(3)]
    local += [pltpu.make_async_copy(q_hbm, q_buf, local_sem.at[6])]
    for copy in local:
        copy.start()

    t_row = lax.broadcasted_iota(jnp.int32, (tokens, tokens), 0)
    t_col = lax.broadcasted_iota(jnp.int32, (tokens, tokens), 1)

    def as_row(column):
        return jnp.sum(jnp.where(t_row == t_col, column, 0), axis=0, keepdims=True)

    ids = ids_in[...]
    probs = prob_in[...]
    id0, id1 = ids[:, 0:1], ids[:, 1:2]
    e_col = lax.broadcasted_iota(jnp.int32, (tokens, n_exp), 1)
    e_row = lax.broadcasted_iota(jnp.int32, (n_exp, tokens), 0)
    named_col = jnp.where((e_col == id0) | (e_col == id1), 1.0, 0.0).astype(F32)
    named_row = jnp.where((e_row == as_row(id0)) | (e_row == as_row(id1)), 1.0, 0.0).astype(F32)
    before = jnp.where(t_col < t_row, 1.0, 0.0).astype(BF16)
    after = jnp.where(t_row < t_col, 1.0, 0.0).astype(BF16)
    rank_col = jnp.dot(before, named_col.astype(BF16), preferred_element_type=F32)
    rank_row = jnp.dot(named_row.astype(BF16), after, preferred_element_type=F32)
    weight_col = jnp.where(e_col == id0, probs[:, 0:1], 0.0) + jnp.where(e_col == id1, probs[:, 1:2], 0.0)
    place_row = lax.broadcasted_iota(jnp.int32, (cap, tokens), 0).astype(F32)
    place_col = lax.broadcasted_iota(jnp.int32, (tokens, cap), 1).astype(F32)
    x = x_in[...]
    for e in range(n_exp):
        chosen = jnp.where(place_row == rank_row[e : e + 1, :], named_row[e : e + 1, :], 0.0)
        rows_out[e] = jnp.dot(chosen.astype(BF16), x, preferred_element_type=F32).astype(BF16)
        back = jnp.where(place_col == rank_col[:, e : e + 1], named_col[:, e : e + 1], 0.0)
        pick[e] = back.astype(BF16)
        gates[e] = weight_col[:, e : e + 1]

    def x_out(d):
        there = (mine + d) % n_exp
        return send(rows_out.at[there], rows_in.at[mine], x_send.at[there], x_recv.at[mine], {"exp": there})

    def x_arrival(d):
        source = (mine + d) % n_exp
        return send(rows_out.at[source], rows_in.at[source], x_send.at[source], x_recv.at[source], {"exp": source})

    for d in range(1, n_exp):
        x_out(d).start()
    rows_in[mine] = rows_out[mine]

    for d in range(1, n_z):
        for j in range(3):
            kv_pass(d, j).wait_recv()
            kv_pass(d, j).start()

    def kv_from_mate(d, j):
        slot = (z + d) % n_z * 2 + 1 - core
        return send(kv_slot(j, slot), kv_slot(j, slot), kv_swap.at[slot // 2, j], kv_recv.at[slot, j], {"ctx": mate})

    for d in range(n_z):
        for j in range(3):
            kv_from_mate(d, j).wait_recv()
    for copy in local[3:]:
        copy.wait()

    own_segment = jnp.sum(
        jnp.where(t_row == t_col, jnp.broadcast_to(seg_buf[me], (tokens, tokens)), 0), axis=1, keepdims=True
    )
    source_segment = jnp.where(own_segment % 2 == 1, own_segment - 1, own_segment)
    for c in range(n_ctx):
        theirs = seg_buf[c]
        allowed = (t_col + c * tokens <= t_row + me * tokens) & (
            (theirs == own_segment) | (theirs == source_segment)
        )
        bias[:, c * tokens : (c + 1) * tokens] = jnp.where(allowed, 0.0, -1e30)

    def relay(s, k):
        for side in (0, 1):
            origin = z - s if side else z + s
            slot = origin * 2 + core

            @pl.when((origin >= 0) & (origin < n_z))
            def _():
                here = piece(k, slot)
                w_mate(here, origin, slot, k).wait_recv()

                @pl.when(has_side(side))
                def _():
                    w_side(side, here, origin, slot, k).start()

                w_mate(here, origin, slot, k).start()

    scale = HEAD_SIZE ** -0.5 * math.log2(math.e)

    def attend(g, carry):
        lanes = pl.ds(pl.multiple_of(g * HEAD_SIZE, HEAD_SIZE), HEAD_SIZE)

        def heads(i, inner):
            for u in range(HEADS_AT_ONCE):
                head = g * group + i * HEADS_AT_ONCE + u
                at = pl.ds(pl.multiple_of(head * HEAD_SIZE, HEAD_SIZE), HEAD_SIZE)
                scores = lax.dot_general(
                    q_buf[:, at], k_buf[:, lanes], (((1,), (1,)), ((), ())), preferred_element_type=F32
                )
                scores = scores * scale + bias[...]
                peak = jnp.max(scores, axis=1, keepdims=True)
                power = jnp.exp2(scores - peak)
                share = 1.0 / jnp.sum(power, axis=1, keepdims=True)
                ctx_buf[:, at] = jnp.dot(
                    (power * share).astype(BF16), v_buf[:, lanes], preferred_element_type=F32
                ).astype(BF16)
            return inner

        lax.fori_loop(0, group // HEADS_AT_ONCE, heads, 0)

        for k in range(2):
            @pl.when(g == 2 * k)
            def _():
                relay(1, k)

        return carry

    lax.fori_loop(0, KEY_HEAD_COUNT, attend, 0)
    ctx_copy = pltpu.make_async_copy(ctx_buf, ctx_out, out_sem.at[0])
    ctx_copy.start()

    for d in range(1, n_exp):
        x_arrival(d).wait_recv()
    for copy in local[:3]:
        copy.wait()

    def hidden_of(origin):
        other = origin * 2 + 1 - core
        for k in range(2):
            w_mate(piece(k, other), origin, other, k).wait_recv()
        inputs = rows_in[...].reshape(n_exp * cap, width)
        both = pl.ds(origin * 2, 2)
        gate_w = weights[0, both].reshape(-1, width)
        up_w = weights[1, both].reshape(-1, width)
        gate = lax.dot_general(inputs, gate_w, (((1,), (1,)), ((), ())), preferred_element_type=F32)
        up = lax.dot_general(inputs, up_w, (((1,), (1,)), ((), ())), preferred_element_type=F32)
        hidden[origin] = (gate / (1.0 + jnp.exp(-gate)) * up).astype(BF16)

    def both_sides(s, what):
        def one(side, inner):
            origin = z + s - 2 * s * side

            @pl.when((origin >= 0) & (origin < n_z))
            def _():
                what(origin)

            return inner

        lax.fori_loop(0, 2, one, 0)

    hidden_of(z)

    def far(s, carry):
        @pl.when(s == n_z - 1)
        def _():
            for k in range(2, PIECES):
                share_own(k)

        @pl.when(s > 1)
        def _():
            for k in range(2):
                relay(s, k)

        both_sides(s, hidden_of)
        return carry

    lax.fori_loop(1, n_z, far, 0)
    hidden_all[...] = jnp.concatenate([hidden[o] for o in range(n_z)], axis=1)

    def r_out(d, cb):
        there = (mine + d) % n_exp
        at = pl.ds(cb * columns, columns)
        return send(
            result.at[there, :, at], returned.at[mine, :, at],
            r_send.at[there, cb], r_recv.at[mine, cb], {"exp": there},
        )

    def r_arrival(d, cb):
        source = (mine + d) % n_exp
        at = pl.ds(cb * columns, columns)
        return send(
            result.at[source, :, at], returned.at[source, :, at],
            r_send.at[source, cb], r_recv.at[source, cb], {"exp": source},
        )

    for cb in range(COLUMN_BLOCKS):
        k = cb + 2

        def pass_on(s, carry):
            relay(s, k)
            return carry

        lax.fori_loop(1, n_z, pass_on, 0)

        def from_mate(origin, carry):
            other = origin * 2 + 1 - core
            w_mate(piece(k, other), origin, other, k).wait_recv()
            return carry

        lax.fori_loop(0, n_z, from_mate, 0)
        at = pl.ds(cb * columns, columns)
        down_w = weights[2, :, :, at].reshape(-1, columns)
        out = jnp.dot(hidden_all[...], down_w, preferred_element_type=F32)
        result[:, :, at] = out.astype(BF16).reshape(n_exp, cap, columns)
        for d in range(1, n_exp):
            r_out(d, cb).start()
    for cb in range(COLUMN_BLOCKS):
        at = pl.ds(cb * columns, columns)
        mix = gates[mine] * jnp.dot(pick[mine], result[mine, :, at], preferred_element_type=F32)
        for d in range(1, n_exp):
            r_arrival(d, cb).wait_recv()
            source = (mine + d) % n_exp
            mix += gates[source] * jnp.dot(pick[source], returned[source, :, at], preferred_element_type=F32)
        mix_buf[:, at] = mix.astype(BF16)
    mix_copy = pltpu.make_async_copy(mix_buf, mix_out, out_sem.at[1])
    mix_copy.start()

    for d in range(1, n_z):
        for j in range(3):
            kv_out(d, j).wait_send()
    for d in range(n_z):
        for j in range(3):
            kv_pass(d, j).wait_send()
    for k in range(PIECES):
        for side in (0, 1):
            @pl.when(has_side(side))
            def _():
                w_side(side, own_piece(k), z, me, k).wait_send()
        w_mate(own_piece(k), z, me, k).wait_send()

    def sent(s, carry):
        for k in range(PIECES):
            for side in (0, 1):
                origin = z - s if side else z + s
                slot = origin * 2 + core

                @pl.when((origin >= 0) & (origin < n_z))
                def _():
                    here = piece(k, slot)

                    @pl.when(has_side(side))
                    def _():
                        w_side(side, here, origin, slot, k).wait_send()

                    w_mate(here, origin, slot, k).wait_send()
        return carry

    lax.fori_loop(1, n_z, sent, 0)
    for d in range(1, n_exp):
        x_out(d).wait_send()
        for cb in range(COLUMN_BLOCKS):
            r_out(d, cb).wait_send()
    ctx_copy.wait()
    mix_copy.wait()


def on_device(
    n_ctx, n_exp,
    queries, key_head_vectors, value_head_vectors, segment_ids,
    normed, expert_ids, gate_probs, gate_weight, up_weight, down_weight,
):
    tokens, q_width = queries.shape[1:]
    kv_width = key_head_vectors.shape[2]
    width = normed.shape[2]
    hidden = gate_weight.shape[1]
    most = tokens * expert_ids.shape[2] * 5 // (4 * n_exp)
    cap = -(-most // 16) * 16
    span = n_ctx * tokens
    n_z = n_ctx // 2
    dma = pltpu.SemaphoreType.DMA
    hbm = pl.BlockSpec(memory_space=pl.ANY)
    vmem = pl.BlockSpec(memory_space=pltpu.VMEM)
    context, mixture = pl.pallas_call(
        functools.partial(kernel, n_ctx, n_exp, cap),
        out_shape=(
            jax.ShapeDtypeStruct((tokens, q_width), BF16),
            jax.ShapeDtypeStruct((tokens, width), BF16),
        ),
        in_specs=[hbm, hbm, hbm, vmem, vmem, vmem, vmem, hbm, hbm, hbm],
        out_specs=(hbm, hbm),
        scratch_shapes=[
            pltpu.VMEM((tokens, q_width), BF16),
            pltpu.VMEM((span, kv_width), BF16),
            pltpu.VMEM((span, kv_width), BF16),
            pltpu.VMEM((n_ctx, 1, tokens), jnp.int32),
            pltpu.VMEM((tokens, span), F32),
            pltpu.VMEM((tokens, q_width), BF16),
            pltpu.VMEM((3, n_ctx, hidden, width), BF16),
            pltpu.VMEM((n_exp, cap, width), BF16),
            pltpu.VMEM((n_exp, cap, width), BF16),
            pltpu.VMEM((n_z, n_exp * cap, 2 * hidden), BF16),
            pltpu.VMEM((n_exp * cap, n_ctx * hidden), BF16),
            pltpu.VMEM((n_exp, cap, width), BF16),
            pltpu.VMEM((n_exp, cap, width), BF16),
            pltpu.VMEM((n_exp, tokens, cap), BF16),
            pltpu.VMEM((n_exp, tokens, 1), F32),
            pltpu.VMEM((tokens, width), BF16),
            dma((7,)),
            dma((n_z, 3)),
            dma((n_z, 3)),
            dma((n_ctx, 3)),
            dma((n_z, PIECES)),
            dma((n_z, PIECES)),
            dma((n_z, PIECES)),
            dma((n_ctx, PIECES)),
            dma((n_exp,)),
            dma((n_exp,)),
            dma((n_exp, COLUMN_BLOCKS)),
            dma((n_exp, COLUMN_BLOCKS)),
            dma((2,)),
        ],
        compiler_params=pltpu.CompilerParams(
            collective_id=0, has_side_effects=True, vmem_limit_bytes=60 * 1024 * 1024
        ),
        name="layer",
    )(
        queries[0], key_head_vectors[0], value_head_vectors[0], segment_ids,
        normed[0], expert_ids[0], gate_probs[0], gate_weight[0], up_weight[0], down_weight[0],
    )
    return context[None], mixture[None]


def solution(mesh):
    rows = P("exp", "ctx", None)
    in_specs = (rows, rows, rows, P("exp", "ctx"), rows, rows, rows, rows, rows, rows)
    return jax.shard_map(
        functools.partial(on_device, mesh.shape["ctx"], mesh.shape["exp"]),
        mesh=mesh, in_specs=in_specs, out_specs=(rows, rows), check_vma=False,
    )
```
